32 devices in a mesh: panel: 16 (over z, y, x), obs: 2 (over core).
Axes of the slice: x: 2, y: 2, z: 4, core: 2. Of those that a mesh axis runs over, the one named last changes fastest.
Arguments:
- donor: bfloat16 [128, 125, 4, 256], P('panel', None, None, 'obs'), may hold values from -6 to 6
- donor_elem: int32 [2048], P('obs'), may hold values from 0 to 255, as said below
- local_coords: float32 [3, 2048], P(None, 'obs'), may hold values from -1 to 1
- owner: int32 [2048], replicated, may hold values from 0 to 15, as said below
- weights: bfloat16 [256, 4, 4, 2048], P('obs', None, None, 'panel'), may hold values from -0.03125 to 0.03125
- offsets: int32 [2, 16], P('obs', 'panel'), may hold values from 0 to 64
Outputs:
- pressure: float32 [128, 256], P('panel', 'obs')
The draws below stay inside these ranges and needn't reach their ends.
Inputs may be any that keep to these rules, and one draw needn't show every extreme that they name: `donor_elem`: point i lies in a donor element of the i // 1024-th block of 128 elements. Every owner owns exactly 128 points. Within each of the 2 aligned blocks of 1024 points an owner appears either 80 times or 128 / 2 - 128 / 8 times, and exactly one block holds 80 of its points.
All inputs are finite; a program needn't handle non-finite values.
Results may differ from the reference program's by a relative error of at most 0.0029.
Values may be sent and summed in bfloat16 or wider, within the bound.
No kernel may reach another device: no remote copies, remote signals or barrier semaphores. Data moves between devices by JAX's collectives and lax.ppermute only.
A program may use at most 64 MiB of HBM per device.

```python
import jax
import jax.numpy as jnp
from jax import lax

PS = 128
ELEMS_DEV = 128
QUANT = 4
NODES = 125
BAND = 4
OBLK = 128
PTILE = 128
TW = 128
MAXOFF = 64
P_ALL = 2048
ELEMS = 256
OBSERVERS = 256
N_PANEL = 16
N_OBS = 2


def draw_donor_elem(key, part):
    share_size = P_ALL // N_OBS
    picks = jax.random.randint(key, (P_ALL,), 0, ELEMS_DEV)
    share_ids = jnp.arange(P_ALL, dtype=jnp.int32) // share_size
    return (share_ids * ELEMS_DEV + picks).astype(jnp.int32)


def shuffle_row(row_key, row_values):
    return row_values[jax.random.permutation(row_key, row_values.shape[0])]


def draw_owner(key, part):
    share_size = P_ALL // N_OBS
    mean_count = PS // N_OBS
    lift = mean_count // 4
    key_shift = jax.random.fold_in(key, 11)
    key_order = jax.random.fold_in(key, 23)
    rotation = jax.random.permutation(key_shift, N_PANEL) % N_OBS
    share_ids = jnp.arange(N_OBS, dtype=jnp.int32)
    phase = (share_ids[:, None] + rotation[None, :]) % N_OBS
    counts = jnp.where(phase == 0, mean_count + (N_OBS - 1) * lift, mean_count - lift)
    bounds = jnp.cumsum(counts, axis=1)
    slot_ids = jnp.arange(share_size, dtype=jnp.int32)
    sorted_owner = jnp.sum((bounds[:, None, :] <= slot_ids[None, :, None]).astype(jnp.int32), axis=2)
    row_keys = jax.random.split(key_order, N_OBS)
    mixed = jax.vmap(shuffle_row)(row_keys, sorted_owner)
    return mixed.reshape(-1).astype(jnp.int32)


def draw_offsets(key, part):
    block_rows = OBSERVERS // OBLK
    tile_cols = P_ALL // PTILE
    key_values = jax.random.fold_in(key, 5)
    key_spots = jax.random.fold_in(key, 7)
    values = jax.random.randint(key_values, (block_rows * tile_cols,), 0, MAXOFF + 1)
    spots = jax.random.permutation(key_spots, block_rows * tile_cols)
    values = values.at[spots[0]].set(MAXOFF)
    values = values.at[spots[1]].set(0)
    return values.reshape(block_rows, tile_cols).astype(jnp.int32)


def shard_levels(stream_key, shape, shards, least, high):
    gain = 1.0
    for axis_at, parts in shards:
        draws = jax.random.uniform(jax.random.fold_in(jax.random.fold_in(stream_key, 6), axis_at), (parts,), jnp.float32, least / len(shards), high / len(shards))
        gain = gain * jnp.repeat(jnp.exp(draws), shape[axis_at] // parts).reshape((-1,) + (1,) * (len(shape) - 1 - axis_at))
    return gain


def scatter_about(stream_key, shape, spread, most, cuts=(), kind=jnp.bfloat16):
    result = spread * jax.random.normal(stream_key, shape, jnp.float32)
    if cuts:
        result = result * shard_levels(stream_key, shape, cuts, -0.22, 0.18)
    return jnp.clip(result, -most, most).astype(kind)


def setup_inputs(seed: int = 0) -> dict:
    key_list = jax.random.split(jax.random.key(seed), 7)
    donor = scatter_about(key_list[0], (TW, NODES, QUANT, ELEMS), 1.0, 6.0, ((0, 16), (3, 2)))
    donor_elem = draw_donor_elem(jax.random.fold_in(key_list[6], 71), 0)
    local_coords = jnp.clip(jax.random.uniform(key_list[2], (3, P_ALL), jnp.float32, -1.0, 1.0) * shard_levels(key_list[2], (3, P_ALL), ((1, 2),), -0.4, 0.0), -1.0, 1.0)
    owner = draw_owner(jax.random.fold_in(key_list[6], 71), 0)
    weights = scatter_about(key_list[4], (OBSERVERS, BAND, QUANT, P_ALL), (P_ALL * QUANT * BAND) ** -0.5, 0.03125, ((0, 2), (3, 16)))
    offsets = draw_offsets(jax.random.fold_in(key_list[6], 71), 0)
    return {"donor": donor, "donor_elem": donor_elem, "local_coords": local_coords, "owner": owner, "weights": weights, "offsets": offsets}


NODE_SPOTS = (-1.0, -0.5, 0.0, 0.5, 1.0)


def lagrange_table(coords):
    factors = []
    for direction in range(3):
        coord_row = coords[direction]
        columns = []
        for node_one in range(5):
            weighting = jnp.ones_like(coord_row)
            for node_two in range(5):
                if node_two != node_one:
                    weighting = weighting * ((coord_row - NODE_SPOTS[node_two]) / (NODE_SPOTS[node_one] - NODE_SPOTS[node_two]))
            columns.append(weighting)
        factors.append(jnp.stack(columns))
    node_table = factors[0][:, None, None, :] * factors[1][None, :, None, :] * factors[2][None, None, :, :]
    return node_table.reshape(125, coords.shape[1])


def reference(donor, donor_elem, local_coords, owner, weights, offsets):
    node_table = lagrange_table(local_coords)

    def one_time(moment):
        values = jnp.take(moment, donor_elem, axis=2).astype(jnp.float32)
        return jnp.sum(node_table[:, None, :] * values, axis=0).astype(jnp.bfloat16)

    sources = lax.map(one_time, donor)
    order = jnp.argsort(owner, stable=True).astype(jnp.int32)
    ordered = jnp.take(sources, order, axis=2)
    padded = jnp.pad(ordered, ((BAND - 1, 0), (0, 0), (0, 0)))
    time_ids = jnp.arange(TW, dtype=jnp.int32)

    def tile_step(running, tile_id):
        start = (tile_id * PTILE).astype(jnp.int32)
        panel_piece = lax.dynamic_slice_in_dim(padded, start, PTILE, 2)
        stacked = jnp.stack([panel_piece[BAND - 1 - delay:BAND - 1 - delay + TW] for delay in range(BAND)], axis=1)
        flat = stacked.reshape(TW, BAND * QUANT * PTILE).astype(jnp.float32)
        weight_tile = lax.dynamic_slice_in_dim(weights, start, PTILE, 3).reshape(OBSERVERS, BAND * QUANT * PTILE).astype(jnp.float32)
        product = jnp.dot(flat, weight_tile.T, precision=lax.Precision.HIGHEST)
        delays = lax.dynamic_slice_in_dim(offsets, tile_id, 1, 1)[:, 0]
        delay_obs = jnp.repeat(delays, OBLK)
        source_time = time_ids[:, None] - delay_obs[None, :]
        moved = jnp.take_along_axis(product, jnp.clip(source_time, 0, TW - 1), axis=0)
        moved = jnp.where(source_time >= 0, moved, jnp.float32(0.0))
        return running + moved, None

    start_total = jnp.zeros((TW, OBSERVERS), jnp.float32)
    pressure, unused = lax.scan(tile_step, start_total, jnp.arange(P_ALL // PTILE, dtype=jnp.int32))
    return pressure
```

```python
import functools

import jax
import jax.numpy as jnp
from jax import lax
from jax.experimental import pallas as pl
from jax.experimental.pallas import tpu as pltpu
from jax.sharding import PartitionSpec as P

LANES = 128
NODE_SPOTS = (-1.0, -0.5, 0.0, 0.5, 1.0)
VM = pl.BlockSpec(memory_space=pltpu.VMEM)
SM = pl.BlockSpec(memory_space=pltpu.SMEM)
NT = (((1,), (1,)), ((), ()))


def lagrange_rows(coord):
    rows = []
    for one in range(5):
        value = None
        scale = 1.0
        for two in range(5):
            if two != one:
                scale = scale * (NODE_SPOTS[one] - NODE_SPOTS[two])
                factor = coord - NODE_SPOTS[two]
                value = factor if value is None else value * factor
        rows.append(value * (1.0 / scale))
    return rows


def interpolate(shape, donor_ref, elem_ref, coords_ref, out_ref, table_ref, hold_ref):
    times, nodes, quants, elems = shape
    points = coords_ref.shape[1]
    width = 2 * LANES
    rows = nodes * quants
    groups = (rows + 7) // 8
    base = lax.axis_index("obs") * elems
    upper = lax.broadcasted_iota(jnp.int32, (8, width), 0) >= quants
    for tile in range(points // width):
        lanes = slice(tile * width, (tile + 1) * width)
        factors = [lagrange_rows(jnp.broadcast_to(coords_ref[d : d + 1, lanes], (8, width))) for d in range(3)]
        zero = jnp.zeros((8, width), jnp.float32)
        basis = []
        for a in range(5):
            for b in range(5):
                ab = factors[0][a] * factors[1][b]
                for c in range(5):
                    basis.append(ab * factors[2][c])
        padded = [zero] + basis + [zero]
        for m in range(groups):
            table_ref[0, m * 8 : m * 8 + 8, :] = jnp.where(upper, padded[2 * m + 2], padded[2 * m + 1])
            table_ref[1, m * 8 : m * 8 + 8, :] = jnp.where(upper, padded[2 * m + 1], padded[2 * m])
        ids = jnp.broadcast_to(elem_ref[0:1, lanes] - base, (elems, width))
        pick = jnp.where(ids == lax.broadcasted_iota(jnp.int32, (elems, width), 0), 1.0, 0.0).astype(jnp.bfloat16)
        for pair in range(times // 2):
            found = jnp.dot(
                donor_ref[pair * 2 * rows : (pair + 1) * 2 * rows, :], pick, preferred_element_type=jnp.float32
            )
            for odd in range(2):
                first = odd * (2 * rows - groups * 8)
                product = found[first : first + groups * 8, :] * table_ref[odd]
                total = jnp.sum(product.reshape(groups, 8, width), axis=0)
                total = total + pltpu.roll(total, 4, 0)
                for q in range(quants):
                    row = q * times + 2 * pair + odd
                    hold_ref[row : row + 1, lanes] = total[q : q + 1]
    out_ref[...] = hold_ref[...].astype(jnp.bfloat16)


def owned_rows(owner_row, src, n_panel):
    src = src.astype(jnp.float32)
    picked = [jnp.where(owner_row == p, src, 0.0).astype(jnp.bfloat16) for p in range(n_panel)]
    return jnp.concatenate(picked, axis=0)


def spots(pos_row, size):
    hit = lax.broadcasted_iota(jnp.int32, (size, pos_row.shape[1]), 0) == pos_row
    return jnp.where(hit, 1.0, 0.0).astype(jnp.bfloat16)


def place_own(n_panel, n_obs, src_ref, owner_ref, out_ref, pos_ref):
    points = src_ref.shape[1]
    every = owner_ref.shape[1]
    size = every // n_panel
    tiles = every // LANES
    spans = (n_panel, LANES)
    rows_p = lax.broadcasted_iota(jnp.int32, spans, 0)
    hits = [
        jnp.where(rows_p == owner_ref[0:1, c * LANES : (c + 1) * LANES], 1.0, 0.0) for c in range(tiles)
    ]
    left = lax.broadcasted_iota(jnp.int32, (LANES, 2 * LANES), 0)
    right = lax.broadcasted_iota(jnp.int32, (LANES, 2 * LANES), 1)
    count = jnp.where((left < right), 1.0, 0.0).astype(jnp.bfloat16)
    sums = jnp.dot(
        jnp.concatenate(hits, axis=0).astype(jnp.bfloat16), count, preferred_element_type=jnp.float32
    )
    before = jnp.zeros(spans, jnp.float32)
    for c in range(tiles):
        part = sums[c * n_panel : (c + 1) * n_panel]
        rank = jnp.sum(hits[c] * (part[:, :LANES] + before), axis=0, keepdims=True)
        pos_ref[0:1, c * LANES : (c + 1) * LANES] = rank.astype(jnp.int32)
        before = before + part[:, LANES:]
    at = pl.ds(pl.multiple_of(lax.axis_index("obs") * points, points), points)
    out_ref[...] = lax.dot_general(
        owned_rows(owner_ref[0:1, at], src_ref[...], n_panel),
        spots(pos_ref[0:1, at], size),
        NT,
        preferred_element_type=jnp.float32,
    ).astype(jnp.bfloat16)


def place_rest(n_panel, n_obs, part_ref, pos_ref, owner_ref, *refs):
    out_ref = refs[-1]
    points = refs[0].shape[1]
    size = owner_ref.shape[1] // n_panel
    total = part_ref[...].astype(jnp.float32)
    for step in range(1, n_obs):
        block = lax.rem(lax.axis_index("obs") + (n_obs - step), n_obs)
        at = pl.ds(pl.multiple_of(block * points, points), points)
        total = total + lax.dot_general(
            owned_rows(owner_ref[0:1, at], refs[step - 1][...], n_panel),
            spots(pos_ref[0:1, at], size),
            NT,
            preferred_element_type=jnp.float32,
        )
    out_ref[...] = total.astype(jnp.bfloat16).reshape(out_ref.shape)


def band_sum(quants, band, got_ref, weight_ref, offset_ref, out_ref, lag_ref, shift_ref):
    parts, rows, size = got_ref.shape
    times = rows // quants
    span = parts * times
    values = got_ref[...].astype(jnp.float32)
    flat = jnp.concatenate(
        [values[:, q * times : (q + 1) * times, :].reshape(span, size).astype(jnp.bfloat16) for q in range(quants)],
        axis=1,
    )
    total = None
    for k in range(band):
        one = lax.dot_general(flat, weight_ref[k], NT, preferred_element_type=jnp.float32)
        if k:
            lag_ref[k - 1, 0:8, :] = jnp.zeros((8, one.shape[1]), jnp.float32)
            lag_ref[k - 1, 8 : 8 + span, :] = one
            one = lag_ref[k - 1, 8 - k : 8 - k + span, :]
        total = one if total is None else total + one
    shift_ref[0:span, :] = jnp.zeros_like(total)
    shift_ref[span : 2 * span, :] = total
    out_ref[...] = shift_ref[pl.ds(span - offset_ref[0, 0], span), :].reshape(out_ref.shape)


def body(donor, donor_elem, local_coords, owner, weights, offsets):
    times, nodes, quants, elems = donor.shape
    points = local_coords.shape[1]
    every = owner.shape[0]
    n_panel = lax.axis_size("panel")
    n_obs = lax.axis_size("obs")
    size = every // n_panel
    observers, band = weights.shape[:2]
    rows = times * quants
    sources = pl.pallas_call(
        functools.partial(interpolate, donor.shape),
        out_shape=jax.ShapeDtypeStruct((rows, points), jnp.bfloat16),
        in_specs=[VM, VM, VM],
        out_specs=VM,
        scratch_shapes=[
            pltpu.VMEM((2, 8 * ((nodes * quants + 7) // 8), 2 * LANES), jnp.float32),
            pltpu.VMEM((rows, points), jnp.float32),
        ],
        name="interpolate",
    )(donor.reshape(times * nodes * quants, elems), donor_elem.reshape(1, points), local_coords)
    others = [
        lax.ppermute(sources, "obs", [(s, (s + step) % n_obs) for s in range(n_obs)]) for step in range(1, n_obs)
    ]
    owner_row = owner.reshape(1, every)
    part, pos = pl.pallas_call(
        functools.partial(place_own, n_panel, n_obs),
        out_shape=(
            jax.ShapeDtypeStruct((n_panel * rows, size), jnp.bfloat16),
            jax.ShapeDtypeStruct((1, every), jnp.int32),
        ),
        in_specs=[VM, VM],
        out_specs=(VM, VM),
        name="place_own",
    )(sources, owner_row)
    outgoing = pl.pallas_call(
        functools.partial(place_rest, n_panel, n_obs),
        out_shape=jax.ShapeDtypeStruct((n_panel, rows, size), jnp.bfloat16),
        in_specs=[VM] * (2 + n_obs),
        out_specs=VM,
        name="place_rest",
    )(part, pos, owner_row, *others)
    got = lax.all_to_all(outgoing, "panel", split_axis=0, concat_axis=0, tiled=True)
    weight_rows = weights.transpose(1, 0, 2, 3).reshape(band, observers, quants * size)
    span = n_panel * times
    partial = pl.pallas_call(
        functools.partial(band_sum, quants, band),
        out_shape=jax.ShapeDtypeStruct((n_panel, times, observers), jnp.float32),
        in_specs=[VM, VM, SM],
        out_specs=VM,
        scratch_shapes=[
            pltpu.VMEM((band - 1, 8 + span, observers), jnp.float32),
            pltpu.VMEM((2 * span, observers), jnp.float32),
        ],
        name="band_sum",
    )(got, weight_rows, offsets)
    shares = lax.all_to_all(partial, "panel", split_axis=0, concat_axis=0, tiled=True)
    return jnp.sum(shares, axis=0)


def solution(mesh):
    return jax.shard_map(
        body,
        mesh=mesh,
        in_specs=(
            P("panel", None, None, "obs"),
            P("obs"),
            P(None, "obs"),
            P(),
            P("obs", None, None, "panel"),
            P("obs", "panel"),
        ),
        out_specs=P("panel", "obs"),
        check_vma=False,
    )
```

```python
import functools

import jax
import jax.numpy as jnp
from jax import lax
from jax.experimental import pallas as pl
from jax.experimental.pallas import tpu as pltpu
from jax.sharding import PartitionSpec as P

LANES = 128
SHUFFLED = 36
NODE_SPOTS = (-1.0, -0.5, 0.0, 0.5, 1.0)
VM = pl.BlockSpec(memory_space=pltpu.VMEM)
SM = pl.BlockSpec(memory_space=pltpu.SMEM)
NT = (((1,), (1,)), ((), ()))


def near(x):
    return pltpu.with_memory_space_constraint(x, pltpu.VMEM)


def lagrange_rows(coords):
    rows = []
    for one in range(5):
        value = None
        scale = 1.0
        for two in range(5):
            if two != one:
                scale = scale * (NODE_SPOTS[one] - NODE_SPOTS[two])
                factor = coords - NODE_SPOTS[two]
                value = factor if value is None else value * factor
        rows.append(value * (1.0 / scale))
    return rows


def interpolate(shape, shuffled, n_panel, donor_src, elem_src, coords_src, owner_src, out_ref, pos_ref, chunk_ref, elem_ref, coords_ref, owner_ref, wide_ref, table_ref, hold_ref, sems):
    times, nodes, quants, elems = shape
    points = coords_ref.shape[1]
    width = 2 * LANES
    rows = nodes * quants
    groups = (rows + 7) // 8
    pairs = times // 2
    half = pairs // 2 * 2 * rows
    copies = [
        pltpu.make_async_copy(donor_src.at[pl.ds(0, half), :], chunk_ref.at[pl.ds(0, half), :], sems.at[0]),
        pltpu.make_async_copy(
            donor_src.at[pl.ds(half, times * rows - half), :], chunk_ref.at[pl.ds(half, times * rows - half), :], sems.at[4]
        ),
    ]
    first = pltpu.make_async_copy(coords_src, coords_ref, sems.at[1])
    second = pltpu.make_async_copy(elem_src, elem_ref, sems.at[2])
    third = pltpu.make_async_copy(owner_src, owner_ref, sems.at[3])
    first.start()
    second.start()
    third.start()
    for copy in copies:
        copy.start()
    first.wait()
    second.wait()
    third.wait()
    rank_points(n_panel, owner_ref, pos_ref)
    base = lax.axis_index("obs") * elems
    upper = lax.broadcasted_iota(jnp.int32, (8, width), 0) >= quants
    tables = lagrange_rows(coords_ref[...])
    zero = jnp.zeros((8, width), jnp.float32)
    for tile in range(points // width):
        lanes = slice(tile * width, (tile + 1) * width)
        factors = [
            [jnp.broadcast_to(tables[a][d : d + 1, lanes], (8, width)) for a in range(5)] for d in range(3)
        ]
        ab = [factors[0][n // 5] * factors[1][n % 5] for n in range(25)]
        lasts = factors[2]
        mixed = {(c, (c + 1) % 5): jnp.where(upper, lasts[(c + 1) % 5], lasts[c]) for c in range(5)}
        for odd in range(2):
            for m in range(groups):
                low, high = 2 * m - odd, 2 * m - odd + 1
                if low < 0:
                    value = jnp.where(upper, ab[0] * lasts[0], zero)
                elif high >= nodes:
                    value = jnp.where(upper, zero, ab[-1] * lasts[-1])
                else:
                    front = ab[low // 5]
                    if high // 5 != low // 5:
                        front = jnp.where(upper, ab[high // 5], front)
                    value = front * mixed[(low % 5, high % 5)]
                table_ref[odd, m * 8 : m * 8 + 8, :] = value
        ids = elem_ref[0:1, lanes] - base
        wanted = jnp.broadcast_to(ids, (elems, width))
        pick = jnp.where(wanted == lax.broadcasted_iota(jnp.int32, (elems, width), 0), 1.0, 0.0).astype(jnp.bfloat16)
        for pair in range(pairs):
            if tile == 0 and pair % (pairs // 2) == 0:
                copies[pair // (pairs // 2)].wait()
                if shuffled:
                    for p in range(pair, pair + pairs // 2):
                        wide_ref[p] = chunk_ref[2 * rows * p : 2 * rows * p + 8 * shuffled, :].astype(jnp.float32)
            found = jnp.dot(
                chunk_ref[2 * rows * pair + 8 * shuffled : 2 * rows * (pair + 1), :], pick, preferred_element_type=jnp.float32)
            if shuffled:
                halves = [
                    jnp.take_along_axis(
                        wide_ref[pair],
                        jnp.broadcast_to(ids[:, h * LANES : (h + 1) * LANES], (8 * shuffled, LANES)),
                        axis=1,
                        mode="promise_in_bounds",
                    )
                    for h in range(2)
                ]
                found = jnp.concatenate([jnp.concatenate(halves, axis=1), found], axis=0)
            for odd in range(2):
                start = odd * (2 * rows - groups * 8)
                product = found[start : start + groups * 8, :] * table_ref[odd]
                total = jnp.sum(product.reshape(groups, 8, width), axis=0)
                total = total + pltpu.roll(total, 4, 0)
                for q in range(quants):
                    row = q * times + 2 * pair + odd
                    hold_ref[row : row + 1, lanes] = total[q : q + 1]
    out_ref[...] = hold_ref[...].astype(jnp.bfloat16)


def place(owner_row, pos_row, src, n_panel, size):
    src = src.astype(jnp.float32)
    half = lax.shift_right_logical(owner_row, 1)
    picked = [jnp.where(half == p, src, 0.0).astype(jnp.bfloat16) for p in range(n_panel // 2)]
    spot = pos_row + (owner_row - 2 * half) * size
    hit = lax.broadcasted_iota(jnp.int32, (2 * size, spot.shape[1]), 0) == spot
    hot = jnp.where(hit, 1.0, 0.0).astype(jnp.bfloat16)
    return lax.dot_general(jnp.concatenate(picked, axis=0), hot, NT, preferred_element_type=jnp.float32)


def rank_points(n_panel, owner_ref, pos_ref):
    every = owner_ref.shape[1]
    tiles = every // LANES
    spans = (n_panel, LANES)
    rows_p = lax.broadcasted_iota(jnp.int32, spans, 0)
    hits = [
        jnp.where(rows_p == owner_ref[0:1, c * LANES : (c + 1) * LANES], 1.0, 0.0) for c in range(tiles)
    ]
    left = lax.broadcasted_iota(jnp.int32, (LANES, 2 * LANES), 0)
    right = lax.broadcasted_iota(jnp.int32, (LANES, 2 * LANES), 1)
    count = jnp.where((left < right), 1.0, 0.0).astype(jnp.bfloat16)
    sums = jnp.dot(
        jnp.concatenate(hits, axis=0).astype(jnp.bfloat16), count, preferred_element_type=jnp.float32
    )
    before = jnp.zeros(spans, jnp.float32)
    for c in range(tiles):
        part = sums[c * n_panel : (c + 1) * n_panel]
        rank = jnp.sum(hits[c] * (part[:, :LANES] + before), axis=0, keepdims=True)
        pos_ref[0:1, c * LANES : (c + 1) * LANES] = rank.astype(jnp.int32)
        before = before + part[:, LANES:]


def place_own(n_panel, src_ref, owner_ref, pos_ref, weight_ref, out_ref, sorted_ref, wide_ref):
    points = src_ref.shape[1]
    size = owner_ref.shape[1] // n_panel
    band, observers, width = sorted_ref.shape
    quants = width // size
    wide_ref[...] = weight_ref[...].astype(jnp.float32)
    for k in range(band):
        for q in range(quants):
            lane = pl.ds(k * quants + q, observers, stride=band * quants)
            sorted_ref[k, :, q * size : (q + 1) * size] = wide_ref[lane, :].astype(jnp.bfloat16)
    at = pl.ds(pl.multiple_of(lax.axis_index("obs") * points, points), points)
    out_ref[...] = place(owner_ref[0:1, at], pos_ref[0:1, at], src_ref[...], n_panel, size).astype(jnp.bfloat16)


def place_rest(n_panel, n_obs, part_ref, owner_ref, pos_ref, offset_ref, *refs):
    others, (out_ref, delay_ref) = refs[:-2], refs[-2:]
    rows, points = others[0].shape
    size = owner_ref.shape[1] // n_panel
    delay_ref[...] = jnp.full(delay_ref.shape, offset_ref[0, 0].astype(jnp.float32))
    total = part_ref[...].astype(jnp.float32)
    for step in range(1, n_obs):
        block = lax.rem(lax.axis_index("obs") + (n_obs - step), n_obs)
        at = pl.ds(pl.multiple_of(block * points, points), points)
        total = total + place(owner_ref[0:1, at], pos_ref[0:1, at], others[step - 1][...], n_panel, size)
    total = total.astype(jnp.bfloat16)
    for p in range(n_panel):
        out_ref[p] = total[p // 2 * rows : (p // 2 + 1) * rows, p % 2 * size : (p % 2 + 1) * size]


def band_sum(quants, band, got_ref, weight_ref, delay_ref, out_ref, lag_ref, shift_ref):
    parts, rows, size = got_ref.shape
    times = rows // quants
    span = parts * times
    values = got_ref[...].astype(jnp.float32)
    flat = jnp.concatenate(
        [values[:, q * times : (q + 1) * times, :].reshape(span, size).astype(jnp.bfloat16) for q in range(quants)],
        axis=1,
    )
    total = None
    for k in range(band):
        one = lax.dot_general(flat, weight_ref[k], NT, preferred_element_type=jnp.float32)
        if k:
            lag_ref[k - 1, 0:8, :] = jnp.zeros((8, one.shape[1]), jnp.float32)
            lag_ref[k - 1, 8 : 8 + span, :] = one
            one = lag_ref[k - 1, 8 - k : 8 - k + span, :]
        total = one if total is None else total + one
    shift_ref[0:span, :] = jnp.zeros_like(total)
    shift_ref[span : 2 * span, :] = total
    out_ref[...] = shift_ref[pl.ds(span - jnp.max(delay_ref[...]).astype(jnp.int32), span), :].reshape(out_ref.shape)


def body(donor, donor_elem, local_coords, owner, weights, offsets):
    times, nodes, quants, elems = donor.shape
    points = local_coords.shape[1]
    every = owner.shape[0]
    n_panel = lax.axis_size("panel")
    n_obs = lax.axis_size("obs")
    size = every // n_panel
    observers, band = weights.shape[:2]
    rows = times * quants
    owner_row = owner.reshape(1, every)
    sources, pos = pl.pallas_call(
        functools.partial(interpolate, donor.shape, SHUFFLED, n_panel),
        out_shape=(pltpu.VMEM((rows, points), jnp.bfloat16), pltpu.VMEM((1, every), jnp.int32)),
        in_specs=[pl.BlockSpec(memory_space=pl.ANY)] * 4,
        out_specs=(VM, VM),
        scratch_shapes=[
            pltpu.VMEM((times * nodes * quants, elems), jnp.bfloat16),
            pltpu.VMEM((1, points), jnp.int32),
            pltpu.VMEM(local_coords.shape, jnp.float32),
            pltpu.VMEM((1, every), jnp.int32),
            pltpu.VMEM((times // 2, 8 * max(SHUFFLED, 1), elems), jnp.float32),
            pltpu.VMEM((2, 8 * ((nodes * quants + 7) // 8), 2 * LANES), jnp.float32),
            pltpu.VMEM((rows, points), jnp.float32),
            pltpu.SemaphoreType.DMA((5,)),
        ],
        name="interpolate",
    )(donor.reshape(times * nodes * quants, elems), donor_elem.reshape(1, points), local_coords, owner_row)
    others = [
        lax.ppermute(sources, "obs", [(s, (s + step) % n_obs) for s in range(n_obs)]) for step in range(1, n_obs)
    ]
    part, weight_rows = pl.pallas_call(
        functools.partial(place_own, n_panel),
        out_shape=(
            pltpu.VMEM((n_panel // 2 * rows, 2 * size), jnp.bfloat16),
            pltpu.VMEM((band, observers, quants * size), jnp.bfloat16),
        ),
        in_specs=[VM, VM, VM, VM],
        out_specs=(VM, VM),
        scratch_shapes=[pltpu.VMEM((observers * band * quants, size), jnp.float32)],
        name="place_own",
    )(near(sources), near(owner_row), near(pos), near(weights.reshape(observers * band * quants, size)))
    outgoing, delay = pl.pallas_call(
        functools.partial(place_rest, n_panel, n_obs),
        out_shape=(pltpu.VMEM((n_panel, rows, size), jnp.bfloat16), pltpu.VMEM((1, LANES), jnp.float32)),
        in_specs=[VM, VM, VM, SM] + [VM] * (n_obs - 1),
        out_specs=(VM, VM),
        name="place_rest",
    )(near(part), near(owner_row), near(pos), offsets, *[near(x) for x in others])
    got = lax.all_to_all(outgoing, "panel", split_axis=0, concat_axis=0, tiled=True)
    span = n_panel * times
    partial = pl.pallas_call(
        functools.partial(band_sum, quants, band),
        out_shape=pltpu.VMEM((n_panel, times, observers), jnp.float32),
        in_specs=[VM, VM, VM],
        out_specs=VM,
        scratch_shapes=[
            pltpu.VMEM((band - 1, 8 + span, observers), jnp.float32),
            pltpu.VMEM((2 * span, observers), jnp.float32),
        ],
        name="band_sum",
    )(near(got), near(weight_rows), near(delay))
    shares = lax.all_to_all(partial, "panel", split_axis=0, concat_axis=0, tiled=True)
    return jnp.sum(shares, axis=0)


def solution(mesh):
    return jax.shard_map(
        body,
        mesh=mesh,
        in_specs=(
            P("panel", None, None, "obs"),
            P("obs"),
            P(None, "obs"),
            P(),
            P("obs", None, None, "panel"),
            P("obs", "panel"),
        ),
        out_specs=P("panel", "obs"),
        check_vma=False,
    )
```

```python
import functools

import jax
import jax.numpy as jnp
from jax import lax
from jax.experimental import pallas as pl
from jax.experimental.pallas import tpu as pltpu
from jax.sharding import PartitionSpec as P

LANES = 128
SHUFFLED = 36
NODE_SPOTS = (-1.0, -0.5, 0.0, 0.5, 1.0)
VM = pl.BlockSpec(memory_space=pltpu.VMEM)
SM = pl.BlockSpec(memory_space=pltpu.SMEM)
NT = (((1,), (1,)), ((), ()))


def near(x):
    return pltpu.with_memory_space_constraint(x, pltpu.VMEM)


def lagrange_rows(coords):
    rows = []
    for one in range(5):
        value = None
        scale = 1.0
        for two in range(5):
            if two != one:
                scale = scale * (NODE_SPOTS[one] - NODE_SPOTS[two])
                factor = coords - NODE_SPOTS[two]
                value = factor if value is None else value * factor
        rows.append(value * (1.0 / scale))
    return rows


def interpolate(shape, shuffled, n_panel, donor_src, elem_src, coords_src, owner_src, out_ref, pos_ref, chunk_ref, elem_ref, coords_ref, owner_ref, wide_ref, table_ref, hold_ref, sems):
    times, nodes, quants, elems = shape
    points = coords_ref.shape[1]
    width = 2 * LANES
    rows = nodes * quants
    groups = (rows + 7) // 8
    pairs = times // 2
    half = pairs // 2 * 2 * rows
    copies = [
        pltpu.make_async_copy(donor_src.at[pl.ds(0, half), :], chunk_ref.at[pl.ds(0, half), :], sems.at[0]),
        pltpu.make_async_copy(
            donor_src.at[pl.ds(half, times * rows - half), :], chunk_ref.at[pl.ds(half, times * rows - half), :], sems.at[4]
        ),
    ]
    first = pltpu.make_async_copy(coords_src, coords_ref, sems.at[1])
    second = pltpu.make_async_copy(elem_src, elem_ref, sems.at[2])
    third = pltpu.make_async_copy(owner_src, owner_ref, sems.at[3])
    first.start()
    second.start()
    third.start()
    for copy in copies:
        copy.start()
    first.wait()
    second.wait()
    third.wait()
    rank_points(n_panel, owner_ref, pos_ref)
    base = lax.axis_index("obs") * elems
    upper = lax.broadcasted_iota(jnp.int32, (8, width), 0) >= quants
    tables = lagrange_rows(coords_ref[...])
    zero = jnp.zeros((8, width), jnp.float32)
    for tile in range(points // width):
        lanes = slice(tile * width, (tile + 1) * width)
        factors = [
            [jnp.broadcast_to(tables[a][d : d + 1, lanes], (8, width)) for a in range(5)] for d in range(3)
        ]
        ab = [factors[0][n // 5] * factors[1][n % 5] for n in range(25)]
        lasts = factors[2]
        mixed = {(c, (c + 1) % 5): jnp.where(upper, lasts[(c + 1) % 5], lasts[c]) for c in range(5)}
        for odd in range(2):
            for m in range(groups):
                low, high = 2 * m - odd, 2 * m - odd + 1
                if low < 0:
                    value = jnp.where(upper, ab[0] * lasts[0], zero)
                elif high >= nodes:
                    value = jnp.where(upper, zero, ab[-1] * lasts[-1])
                else:
                    front = ab[low // 5]
                    if high // 5 != low // 5:
                        front = jnp.where(upper, ab[high // 5], front)
                    value = front * mixed[(low % 5, high % 5)]
                table_ref[odd, m * 8 : m * 8 + 8, :] = value
        ids = elem_ref[0:1, lanes] - base
        wanted = jnp.broadcast_to(ids, (elems, width))
        pick = jnp.where(wanted == lax.broadcasted_iota(jnp.int32, (elems, width), 0), 1.0, 0.0).astype(jnp.bfloat16)
        for pair in range(pairs):
            if tile == 0 and pair == 0:
                [copy.wait() for copy in copies]
                if shuffled:
                    for p in range(pairs):
                        wide_ref[p] = chunk_ref[2 * rows * p : 2 * rows * p + 8 * shuffled, :].astype(jnp.float32)
            found = jnp.dot(
                chunk_ref[2 * rows * pair + 8 * shuffled : 2 * rows * (pair + 1), :], pick, preferred_element_type=jnp.float32)
            if shuffled:
                halves = [
                    jnp.take_along_axis(
                        wide_ref[pair],
                        jnp.broadcast_to(ids[:, h * LANES : (h + 1) * LANES], (8 * shuffled, LANES)),
                        axis=1,
                        mode="promise_in_bounds",
                    )
                    for h in range(2)
                ]
                found = jnp.concatenate([jnp.concatenate(halves, axis=1), found], axis=0)
            for odd in range(2):
                start = odd * (2 * rows - groups * 8)
                product = found[start : start + groups * 8, :] * table_ref[odd]
                total = jnp.sum(product.reshape(groups, 8, width), axis=0)
                total = total + pltpu.roll(total, 4, 0)
                for q in range(quants):
                    row = q * times + 2 * pair + odd
                    hold_ref[row : row + 1, lanes] = total[q : q + 1]
    out_ref[...] = hold_ref[...].astype(jnp.bfloat16)


def place(owner_row, pos_row, src, n_panel, size):
    src = src.astype(jnp.float32)
    half = lax.shift_right_logical(owner_row, 1)
    picked = [jnp.where(half == p, src, 0.0).astype(jnp.bfloat16) for p in range(n_panel // 2)]
    spot = pos_row + (owner_row - 2 * half) * size
    hit = lax.broadcasted_iota(jnp.int32, (2 * size, spot.shape[1]), 0) == spot
    hot = jnp.where(hit, 1.0, 0.0).astype(jnp.bfloat16)
    return lax.dot_general(jnp.concatenate(picked, axis=0), hot, NT, preferred_element_type=jnp.float32)


def rank_points(n_panel, owner_ref, pos_ref):
    every = owner_ref.shape[1]
    tiles = every // LANES
    spans = (n_panel, LANES)
    rows_p = lax.broadcasted_iota(jnp.int32, spans, 0)
    hits = [
        jnp.where(rows_p == owner_ref[0:1, c * LANES : (c + 1) * LANES], 1.0, 0.0) for c in range(tiles)
    ]
    left = lax.broadcasted_iota(jnp.int32, (LANES, 2 * LANES), 0)
    right = lax.broadcasted_iota(jnp.int32, (LANES, 2 * LANES), 1)
    count = jnp.where((left < right), 1.0, 0.0).astype(jnp.bfloat16)
    sums = jnp.dot(
        jnp.concatenate(hits, axis=0).astype(jnp.bfloat16), count, preferred_element_type=jnp.float32
    )
    before = jnp.zeros(spans, jnp.float32)
    for c in range(tiles):
        part = sums[c * n_panel : (c + 1) * n_panel]
        rank = jnp.sum(hits[c] * (part[:, :LANES] + before), axis=0, keepdims=True)
        pos_ref[0:1, c * LANES : (c + 1) * LANES] = rank.astype(jnp.int32)
        before = before + part[:, LANES:]


def place_own(n_panel, src_ref, owner_ref, pos_ref, out_ref):
    rows, points = src_ref.shape
    size = owner_ref.shape[1] // n_panel
    at = pl.ds(pl.multiple_of(lax.axis_index("obs") * points, points), points)
    part = place(owner_ref[0:1, at], pos_ref[0:1, at], src_ref[...], n_panel, size).astype(jnp.bfloat16)
    for p in range(n_panel):
        out_ref[p] = part[p // 2 * rows : (p // 2 + 1) * rows, p % 2 * size : (p % 2 + 1) * size]


def sort_weights(got_ref, weight_ref, offset_ref, sorted_ref, delay_ref, wide_ref):
    band, observers, width = sorted_ref.shape
    size = weight_ref.shape[1]
    quants = width // size
    delay_ref[...] = jnp.full(delay_ref.shape, offset_ref[0, 0].astype(jnp.float32))
    wide_ref[...] = weight_ref[...].astype(jnp.float32)
    for k in range(band):
        for q in range(quants):
            lane = pl.ds(k * quants + q, observers, stride=band * quants)
            sorted_ref[k, :, q * size : (q + 1) * size] = wide_ref[lane, :].astype(jnp.bfloat16)


def band_sum(quants, band, weight_ref, delay_ref, *refs):
    got_refs, (out_ref, lag_ref, shift_ref) = refs[:-3], refs[-3:]
    parts, rows, size = got_refs[0].shape
    times = rows // quants
    span = parts * times
    values = sum(ref[...].astype(jnp.float32) for ref in got_refs)
    flat = jnp.concatenate(
        [values[:, q * times : (q + 1) * times, :].reshape(span, size).astype(jnp.bfloat16) for q in range(quants)],
        axis=1,
    )
    total = None
    for k in range(band):
        one = lax.dot_general(flat, weight_ref[k], NT, preferred_element_type=jnp.float32)
        if k:
            lag_ref[k - 1, 0:8, :] = jnp.zeros((8, one.shape[1]), jnp.float32)
            lag_ref[k - 1, 8 : 8 + span, :] = one
            one = lag_ref[k - 1, 8 - k : 8 - k + span, :]
        total = one if total is None else total + one
    shift_ref[0:span, :] = jnp.zeros_like(total)
    shift_ref[span : 2 * span, :] = total
    out_ref[...] = shift_ref[pl.ds(span - jnp.max(delay_ref[...]).astype(jnp.int32), span), :].reshape(out_ref.shape)


def body(donor, donor_elem, local_coords, owner, weights, offsets):
    times, nodes, quants, elems = donor.shape
    points = local_coords.shape[1]
    every = owner.shape[0]
    n_panel = lax.axis_size("panel")
    n_obs = lax.axis_size("obs")
    size = every // n_panel
    observers, band = weights.shape[:2]
    rows = times * quants
    owner_row = owner.reshape(1, every)
    sources, pos = pl.pallas_call(
        functools.partial(interpolate, donor.shape, SHUFFLED, n_panel),
        out_shape=(pltpu.VMEM((rows, points), jnp.bfloat16), pltpu.VMEM((1, every), jnp.int32)),
        in_specs=[pl.BlockSpec(memory_space=pl.ANY)] * 4,
        out_specs=(VM, VM),
        scratch_shapes=[
            pltpu.VMEM((times * nodes * quants, elems), jnp.bfloat16),
            pltpu.VMEM((1, points), jnp.int32),
            pltpu.VMEM(local_coords.shape, jnp.float32),
            pltpu.VMEM((1, every), jnp.int32),
            pltpu.VMEM((times // 2, 8 * max(SHUFFLED, 1), elems), jnp.float32),
            pltpu.VMEM((2, 8 * ((nodes * quants + 7) // 8), 2 * LANES), jnp.float32),
            pltpu.VMEM((rows, points), jnp.float32),
            pltpu.SemaphoreType.DMA((5,)),
        ],
        name="interpolate",
    )(donor.reshape(times * nodes * quants, elems), donor_elem.reshape(1, points), local_coords, owner_row)
    outgoing = pl.pallas_call(
        functools.partial(place_own, n_panel),
        out_shape=pltpu.VMEM((n_panel, rows, size), jnp.bfloat16),
        in_specs=[VM, VM, VM],
        out_specs=VM,
        name="place_own",
    )(near(sources), near(owner_row), near(pos))
    got = lax.all_to_all(outgoing, "panel", split_axis=0, concat_axis=0, tiled=True)
    others = [lax.ppermute(got, "obs", [(s, (s + step) % n_obs) for s in range(n_obs)]) for step in range(1, n_obs)]
    got, offsets = lax.optimization_barrier((got, offsets))
    weight_rows, delay = pl.pallas_call(
        sort_weights,
        out_shape=(
            pltpu.VMEM((band, observers, quants * size), jnp.bfloat16),
            pltpu.VMEM((1, LANES), jnp.float32),
        ),
        in_specs=[VM, VM, SM],
        out_specs=(VM, VM),
        scratch_shapes=[pltpu.VMEM((observers * band * quants, size), jnp.float32)],
        name="sort_weights",
    )(near(got), near(weights.reshape(observers * band * quants, size)), offsets)
    span = n_panel * times
    partial = pl.pallas_call(
        functools.partial(band_sum, quants, band),
        out_shape=pltpu.VMEM((n_panel, times, observers), jnp.float32),
        in_specs=[VM] * (2 + n_obs),
        out_specs=VM,
        scratch_shapes=[
            pltpu.VMEM((band - 1, 8 + span, observers), jnp.float32),
            pltpu.VMEM((2 * span, observers), jnp.float32),
        ],
        name="band_sum",
    )(near(weight_rows), near(delay), near(got), *[near(x) if n_obs == 2 else x for x in others])
    shares = lax.all_to_all(partial, "panel", split_axis=0, concat_axis=0, tiled=True)
    return jnp.sum(shares, axis=0)


def solution(mesh):
    return jax.shard_map(
        body,
        mesh=mesh,
        in_specs=(
            P("panel", None, None, "obs"),
            P("obs"),
            P(None, "obs"),
            P(),
            P("obs", None, None, "panel"),
            P("obs", "panel"),
        ),
        out_specs=P("panel", "obs"),
        check_vma=False,
    )
```

```python
import functools

import jax
import jax.numpy as jnp
from jax import lax
from jax.experimental import pallas as pl
from jax.experimental.pallas import tpu as pltpu
from jax.sharding import PartitionSpec as P

LANES = 128
SHUFFLED = 36
NODE_SPOTS = (-1.0, -0.5, 0.0, 0.5, 1.0)
VM = pl.BlockSpec(memory_space=pltpu.VMEM)
SM = pl.BlockSpec(memory_space=pltpu.SMEM)
NT = (((1,), (1,)), ((), ()))


def near(x):
    return pltpu.with_memory_space_constraint(x, pltpu.VMEM)


def lagrange_rows(coords):
    rows = []
    for one in range(5):
        value = None
        scale = 1.0
        for two in range(5):
            if two != one:
                scale = scale * (NODE_SPOTS[one] - NODE_SPOTS[two])
                factor = coords - NODE_SPOTS[two]
                value = factor if value is None else value * factor
        rows.append(value * (1.0 / scale))
    return rows


def interpolate(shape, shuffled, n_panel, donor_src, elem_src, coords_src, owner_src, out_ref, pos_ref, chunk_ref, elem_ref, coords_ref, owner_ref, wide_ref, table_ref, hold_ref, sems):
    times, nodes, quants, elems = shape
    points = coords_ref.shape[1]
    width = 2 * LANES
    rows = nodes * quants
    groups = (rows + 7) // 8
    pairs = times // 2
    half = pairs // 2 * 2 * rows
    copies = [
        pltpu.make_async_copy(donor_src.at[pl.ds(0, half), :], chunk_ref.at[pl.ds(0, half), :], sems.at[0]),
        pltpu.make_async_copy(
            donor_src.at[pl.ds(half, times * rows - half), :], chunk_ref.at[pl.ds(half, times * rows - half), :], sems.at[4]
        ),
    ]
    first = pltpu.make_async_copy(coords_src, coords_ref, sems.at[1])
    second = pltpu.make_async_copy(elem_src, elem_ref, sems.at[2])
    third = pltpu.make_async_copy(owner_src, owner_ref, sems.at[3])
    first.start()
    second.start()
    third.start()
    for copy in copies:
        copy.start()
    first.wait()
    second.wait()
    third.wait()
    rank_points(n_panel, owner_ref, pos_ref)
    base = lax.axis_index("obs") * elems
    upper = lax.broadcasted_iota(jnp.int32, (8, width), 0) >= quants
    tables = lagrange_rows(coords_ref[...])
    zero = jnp.zeros((8, width), jnp.float32)
    for tile in range(points // width):
        lanes = slice(tile * width, (tile + 1) * width)
        factors = [
            [jnp.broadcast_to(tables[a][d : d + 1, lanes], (8, width)) for a in range(5)] for d in range(3)
        ]
        ab = [factors[0][n // 5] * factors[1][n % 5] for n in range(25)]
        lasts = factors[2]
        mixed = {(c, (c + 1) % 5): jnp.where(upper, lasts[(c + 1) % 5], lasts[c]) for c in range(5)}
        for odd in range(2):
            for m in range(groups):
                low, high = 2 * m - odd, 2 * m - odd + 1
                if low < 0:
                    value = jnp.where(upper, ab[0] * lasts[0], zero)
                elif high >= nodes:
                    value = jnp.where(upper, zero, ab[-1] * lasts[-1])
                else:
                    front = ab[low // 5]
                    if high // 5 != low // 5:
                        front = jnp.where(upper, ab[high // 5], front)
                    value = front * mixed[(low % 5, high % 5)]
                table_ref[odd, m * 8 : m * 8 + 8, :] = value
        ids = elem_ref[0:1, lanes] - base
        wanted = jnp.broadcast_to(ids, (elems, width))
        pick = jnp.where(wanted == lax.broadcasted_iota(jnp.int32, (elems, width), 0), 1.0, 0.0).astype(jnp.bfloat16)
        for pair in range(pairs):
            if tile == 0 and pair == 0:
                [copy.wait() for copy in copies]
                if shuffled:
                    for p in range(pairs):
                        wide_ref[p] = chunk_ref[2 * rows * p : 2 * rows * p + 8 * shuffled, :].astype(jnp.float32)
            found = jnp.dot(
                chunk_ref[2 * rows * pair + 8 * shuffled : 2 * rows * (pair + 1), :], pick, preferred_element_type=jnp.float32)
            if shuffled:
                halves = [
                    jnp.take_along_axis(
                        wide_ref[pair],
                        jnp.broadcast_to(ids[:, h * LANES : (h + 1) * LANES], (8 * shuffled, LANES)),
                        axis=1,
                        mode="promise_in_bounds",
                    )
                    for h in range(2)
                ]
                found = jnp.concatenate([jnp.concatenate(halves, axis=1), found], axis=0)
            for odd in range(2):
                start = odd * (2 * rows - groups * 8)
                product = found[start : start + groups * 8, :] * table_ref[odd]
                total = jnp.sum(product.reshape(groups, 8, width), axis=0)
                total = total + pltpu.roll(total, 4, 0)
                for q in range(quants):
                    row = q * times + 2 * pair + odd
                    hold_ref[row : row + 1, lanes] = total[q : q + 1]
    out_ref[...] = hold_ref[...].astype(jnp.bfloat16)


def place(owner_row, pos_row, src, n_panel, size):
    src = src.astype(jnp.float32)
    half = lax.shift_right_logical(owner_row, 1)
    picked = [jnp.where(half == p, src, 0.0).astype(jnp.bfloat16) for p in range(n_panel // 2)]
    spot = pos_row + (owner_row - 2 * half) * size
    hit = lax.broadcasted_iota(jnp.int32, (2 * size, spot.shape[1]), 0) == spot
    hot = jnp.where(hit, 1.0, 0.0).astype(jnp.bfloat16)
    return lax.dot_general(jnp.concatenate(picked, axis=0), hot, NT, preferred_element_type=jnp.float32)


def rank_points(n_panel, owner_ref, pos_ref):
    every = owner_ref.shape[1]
    tiles = every // LANES
    spans = (n_panel, LANES)
    rows_p = lax.broadcasted_iota(jnp.int32, spans, 0)
    hits = [
        jnp.where(rows_p == owner_ref[0:1, c * LANES : (c + 1) * LANES], 1.0, 0.0) for c in range(tiles)
    ]
    left = lax.broadcasted_iota(jnp.int32, (LANES, 2 * LANES), 0)
    right = lax.broadcasted_iota(jnp.int32, (LANES, 2 * LANES), 1)
    count = jnp.where((left < right), 1.0, 0.0).astype(jnp.bfloat16)
    sums = jnp.dot(
        jnp.concatenate(hits, axis=0).astype(jnp.bfloat16), count, preferred_element_type=jnp.float32
    )
    before = jnp.zeros(spans, jnp.float32)
    for c in range(tiles):
        part = sums[c * n_panel : (c + 1) * n_panel]
        rank = jnp.sum(hits[c] * (part[:, :LANES] + before), axis=0, keepdims=True)
        pos_ref[0:1, c * LANES : (c + 1) * LANES] = rank.astype(jnp.int32)
        before = before + part[:, LANES:]


def place_own(n_panel, src_ref, owner_ref, pos_ref, out_ref):
    rows, points = src_ref.shape
    size = owner_ref.shape[1] // n_panel
    at = pl.ds(pl.multiple_of(lax.axis_index("obs") * points, points), points)
    part = place(owner_ref[0:1, at], pos_ref[0:1, at], src_ref[...], n_panel, size).astype(jnp.bfloat16)
    for p in range(n_panel):
        out_ref[p] = part[p // 2 * rows : (p // 2 + 1) * rows, p % 2 * size : (p % 2 + 1) * size]


def sort_weights(got_ref, weight_ref, offset_ref, sorted_ref, delay_ref, wide_ref):
    band, observers, width = sorted_ref.shape
    size = weight_ref.shape[1]
    quants = width // size
    delay_ref[...] = jnp.full(delay_ref.shape, offset_ref[0, 0].astype(jnp.float32))
    wide_ref[...] = weight_ref[...].astype(jnp.float32)
    for k in range(band):
        for q in range(quants):
            lane = pl.ds(k * quants + q, observers, stride=band * quants)
            sorted_ref[k, :, q * size : (q + 1) * size] = wide_ref[lane, :].astype(jnp.bfloat16)


def band_sum(quants, band, weight_ref, delay_ref, *refs):
    got_refs, (out_ref, lag_ref, shift_ref) = refs[:-3], refs[-3:]
    parts, times, observers = out_ref.shape
    size = got_refs[0].shape[2]
    span = parts * times
    held = [ref[...].astype(jnp.float32) for ref in got_refs]
    if held[0].shape[0] == parts:
        values = sum(held)
    else:
        n_obs = len(held)
        held = [jnp.sum(x.reshape(parts, n_obs, x.shape[1], size), axis=1) for x in held]
        me = lax.axis_index("obs")
        chunks = []
        for c in range(n_obs):
            chunk = held[0]
            for step in range(1, n_obs):
                chunk = jnp.where(lax.rem(me + (n_obs - step), n_obs) == c, held[step], chunk)
            chunks.append(chunk)
        values = jnp.concatenate(chunks, axis=1)
    flat = jnp.concatenate(
        [values[:, q * times : (q + 1) * times, :].reshape(span, size).astype(jnp.bfloat16) for q in range(quants)],
        axis=1,
    )
    total = None
    for k in range(band):
        one = lax.dot_general(flat, weight_ref[k], NT, preferred_element_type=jnp.float32)
        if k:
            lag_ref[k - 1, 0:8, :] = jnp.zeros((8, one.shape[1]), jnp.float32)
            lag_ref[k - 1, 8 : 8 + span, :] = one
            one = lag_ref[k - 1, 8 - k : 8 - k + span, :]
        total = one if total is None else total + one
    shift_ref[0:span, :] = jnp.zeros_like(total)
    shift_ref[span : 2 * span, :] = total
    out_ref[...] = shift_ref[pl.ds(span - jnp.max(delay_ref[...]).astype(jnp.int32), span), :].reshape(out_ref.shape)


def body(donor, donor_elem, local_coords, owner, weights, offsets):
    times, nodes, quants, elems = donor.shape
    points = local_coords.shape[1]
    every = owner.shape[0]
    n_panel = lax.axis_size("panel")
    n_obs = lax.axis_size("obs")
    size = every // n_panel
    observers, band = weights.shape[:2]
    rows = times * quants
    owner_row = owner.reshape(1, every)
    sources, pos = pl.pallas_call(
        functools.partial(interpolate, donor.shape, SHUFFLED, n_panel),
        out_shape=(pltpu.VMEM((rows, points), jnp.bfloat16), pltpu.VMEM((1, every), jnp.int32)),
        in_specs=[pl.BlockSpec(memory_space=pl.ANY)] * 4,
        out_specs=(VM, VM),
        scratch_shapes=[
            pltpu.VMEM((times * nodes * quants, elems), jnp.bfloat16),
            pltpu.VMEM((1, points), jnp.int32),
            pltpu.VMEM(local_coords.shape, jnp.float32),
            pltpu.VMEM((1, every), jnp.int32),
            pltpu.VMEM((times // 2, 8 * max(SHUFFLED, 1), elems), jnp.float32),
            pltpu.VMEM((2, 8 * ((nodes * quants + 7) // 8), 2 * LANES), jnp.float32),
            pltpu.VMEM((rows, points), jnp.float32),
            pltpu.SemaphoreType.DMA((5,)),
        ],
        name="interpolate",
    )(donor.reshape(times * nodes * quants, elems), donor_elem.reshape(1, points), local_coords, owner_row)
    outgoing = pl.pallas_call(
        functools.partial(place_own, n_panel),
        out_shape=pltpu.VMEM((n_panel, rows, size), jnp.bfloat16),
        in_specs=[VM, VM, VM],
        out_specs=VM,
        name="place_own",
    )(near(sources), near(owner_row), near(pos))
    if quants % n_obs == 0:
        outgoing = outgoing.reshape(n_panel * n_obs, rows // n_obs, size)
        got = lax.all_to_all(outgoing, ("panel", "obs"), split_axis=0, concat_axis=0, tiled=True)
    else:
        got = lax.all_to_all(outgoing, "panel", split_axis=0, concat_axis=0, tiled=True)
    others = [lax.ppermute(got, "obs", [(s, (s + step) % n_obs) for s in range(n_obs)]) for step in range(1, n_obs)]
    got, offsets = lax.optimization_barrier((got, offsets))
    weight_rows, delay = pl.pallas_call(
        sort_weights,
        out_shape=(
            pltpu.VMEM((band, observers, quants * size), jnp.bfloat16),
            pltpu.VMEM((1, LANES), jnp.float32),
        ),
        in_specs=[VM, VM, SM],
        out_specs=(VM, VM),
        scratch_shapes=[pltpu.VMEM((observers * band * quants, size), jnp.float32)],
        name="sort_weights",
    )(near(got), near(weights.reshape(observers * band * quants, size)), offsets)
    span = n_panel * times
    partial = pl.pallas_call(
        functools.partial(band_sum, quants, band),
        out_shape=pltpu.VMEM((n_panel, times, observers), jnp.float32),
        in_specs=[VM] * (2 + n_obs),
        out_specs=VM,
        scratch_shapes=[
            pltpu.VMEM((band - 1, 8 + span, observers), jnp.float32),
            pltpu.VMEM((2 * span, observers), jnp.float32),
        ],
        name="band_sum",
    )(near(weight_rows), near(delay), near(got), *[near(x) if n_obs == 2 else x for x in others])
    shares = lax.all_to_all(partial, "panel", split_axis=0, concat_axis=0, tiled=True)
    return jnp.sum(shares, axis=0)


def solution(mesh):
    return jax.shard_map(
        body,
        mesh=mesh,
        in_specs=(
            P("panel", None, None, "obs"),
            P("obs"),
            P(None, "obs"),
            P(),
            P("obs", None, None, "panel"),
            P("obs", "panel"),
        ),
        out_specs=P("panel", "obs"),
        check_vma=False,
    )
```

```python
import functools

import jax
import jax.numpy as jnp
from jax import lax
from jax.experimental import pallas as pl
from jax.experimental.pallas import tpu as pltpu
from jax.sharding import PartitionSpec as P

LANES = 128
SHUFFLED = 36
NODE_SPOTS = (-1.0, -0.5, 0.0, 0.5, 1.0)
VM = pl.BlockSpec(memory_space=pltpu.VMEM)
SM = pl.BlockSpec(memory_space=pltpu.SMEM)
NT = (((1,), (1,)), ((), ()))


def near(x):
    return pltpu.with_memory_space_constraint(x, pltpu.VMEM)


def lagrange_rows(coords):
    rows = []
    for one in range(5):
        value = None
        scale = 1.0
        for two in range(5):
            if two != one:
                scale = scale * (NODE_SPOTS[one] - NODE_SPOTS[two])
                factor = coords - NODE_SPOTS[two]
                value = factor if value is None else value * factor
        rows.append(value * (1.0 / scale))
    return rows


def interpolate(shape, shuffled, n_panel, donor_src, elem_src, coords_src, owner_src, out_ref, pos_ref, chunk_ref, elem_ref, coords_ref, owner_ref, wide_ref, table_ref, hold_ref, sems):
    times, nodes, quants, elems = shape
    points = coords_ref.shape[1]
    width = 2 * LANES
    rows = nodes * quants
    groups = (rows + 7) // 8
    pairs = times // 2
    half = pairs // 2 * 2 * rows
    copies = [
        pltpu.make_async_copy(donor_src.at[pl.ds(0, half), :], chunk_ref.at[pl.ds(0, half), :], sems.at[0]),
        pltpu.make_async_copy(
            donor_src.at[pl.ds(half, times * rows - half), :], chunk_ref.at[pl.ds(half, times * rows - half), :], sems.at[4]
        ),
    ]
    first = pltpu.make_async_copy(coords_src, coords_ref, sems.at[1])
    second = pltpu.make_async_copy(elem_src, elem_ref, sems.at[2])
    third = pltpu.make_async_copy(owner_src, owner_ref, sems.at[3])
    first.start()
    second.start()
    third.start()
    for copy in copies:
        copy.start()
    first.wait()
    second.wait()
    third.wait()
    rank_points(n_panel, owner_ref, pos_ref)
    base = lax.axis_index("obs") * elems
    upper = lax.broadcasted_iota(jnp.int32, (8, width), 0) >= quants
    tables = lagrange_rows(coords_ref[...])
    zero = jnp.zeros((8, width), jnp.float32)
    for tile in range(points // width):
        lanes = slice(tile * width, (tile + 1) * width)
        factors = [
            [jnp.broadcast_to(tables[a][d : d + 1, lanes], (8, width)) for a in range(5)] for d in range(3)
        ]
        ab = [factors[0][n // 5] * factors[1][n % 5] for n in range(25)]
        lasts = factors[2]
        mixed = {(c, (c + 1) % 5): jnp.where(upper, lasts[(c + 1) % 5], lasts[c]) for c in range(5)}
        for odd in range(2):
            for m in range(groups):
                low, high = 2 * m - odd, 2 * m - odd + 1
                if low < 0:
                    value = jnp.where(upper, ab[0] * lasts[0], zero)
                elif high >= nodes:
                    value = jnp.where(upper, zero, ab[-1] * lasts[-1])
                else:
                    front = ab[low // 5]
                    if high // 5 != low // 5:
                        front = jnp.where(upper, ab[high // 5], front)
                    value = front * mixed[(low % 5, high % 5)]
                table_ref[odd, m * 8 : m * 8 + 8, :] = value
        ids = elem_ref[0:1, lanes] - base
        wanted = jnp.broadcast_to(ids, (elems, width))
        pick = jnp.where(wanted == lax.broadcasted_iota(jnp.int32, (elems, width), 0), 1.0, 0.0).astype(jnp.bfloat16)
        for pair in range(pairs):
            if tile == 0 and pair == 0:
                [copy.wait() for copy in copies]
                if shuffled:
                    for p in range(pairs):
                        wide_ref[p] = chunk_ref[2 * rows * p : 2 * rows * p + 8 * shuffled, :].astype(jnp.float32)
            found = jnp.dot(
                chunk_ref[2 * rows * pair + 8 * shuffled : 2 * rows * (pair + 1), :], pick, preferred_element_type=jnp.float32)
            if shuffled:
                halves = [
                    jnp.take_along_axis(
                        wide_ref[pair],
                        jnp.broadcast_to(ids[:, h * LANES : (h + 1) * LANES], (8 * shuffled, LANES)),
                        axis=1,
                        mode="promise_in_bounds",
                    )
                    for h in range(2)
                ]
                found = jnp.concatenate([jnp.concatenate(halves, axis=1), found], axis=0)
            for odd in range(2):
                start = odd * (2 * rows - groups * 8)
                product = found[start : start + groups * 8, :] * table_ref[odd]
                total = jnp.sum(product.reshape(groups, 8, width), axis=0)
                total = total + pltpu.roll(total, 4, 0)
                for q in range(quants):
                    row = q * times + 2 * pair + odd
                    hold_ref[row : row + 1, lanes] = total[q : q + 1]
    out_ref[...] = hold_ref[...].astype(jnp.bfloat16)


def place(owner_row, pos_row, src, n_panel, size):
    src = src.astype(jnp.float32)
    half = lax.shift_right_logical(owner_row, 1)
    picked = [jnp.where(half == p, src, 0.0).astype(jnp.bfloat16) for p in range(n_panel // 2)]
    spot = pos_row + (owner_row - 2 * half) * size
    hit = lax.broadcasted_iota(jnp.int32, (2 * size, spot.shape[1]), 0) == spot
    hot = jnp.where(hit, 1.0, 0.0).astype(jnp.bfloat16)
    return lax.dot_general(jnp.concatenate(picked, axis=0), hot, NT, preferred_element_type=jnp.float32)


def rank_points(n_panel, owner_ref, pos_ref):
    every = owner_ref.shape[1]
    tiles = every // LANES
    spans = (n_panel, LANES)
    rows_p = lax.broadcasted_iota(jnp.int32, spans, 0)
    hits = [
        jnp.where(rows_p == owner_ref[0:1, c * LANES : (c + 1) * LANES], 1.0, 0.0) for c in range(tiles)
    ]
    left = lax.broadcasted_iota(jnp.int32, (LANES, 2 * LANES), 0)
    right = lax.broadcasted_iota(jnp.int32, (LANES, 2 * LANES), 1)
    count = jnp.where((left < right), 1.0, 0.0).astype(jnp.bfloat16)
    sums = jnp.dot(
        jnp.concatenate(hits, axis=0).astype(jnp.bfloat16), count, preferred_element_type=jnp.float32
    )
    before = jnp.zeros(spans, jnp.float32)
    for c in range(tiles):
        part = sums[c * n_panel : (c + 1) * n_panel]
        rank = jnp.sum(hits[c] * (part[:, :LANES] + before), axis=0, keepdims=True)
        pos_ref[0:1, c * LANES : (c + 1) * LANES] = rank.astype(jnp.int32)
        before = before + part[:, LANES:]


def place_own(n_panel, src_ref, owner_ref, pos_ref, out_ref):
    rows, points = src_ref.shape
    size = owner_ref.shape[1] // n_panel
    at = pl.ds(pl.multiple_of(lax.axis_index("obs") * points, points), points)
    part = place(owner_ref[0:1, at], pos_ref[0:1, at], src_ref[...], n_panel, size).astype(jnp.bfloat16)
    for p in range(n_panel):
        out_ref[p] = part[p // 2 * rows : (p // 2 + 1) * rows, p % 2 * size : (p % 2 + 1) * size]


def sort_weights(got_ref, weight_ref, offset_ref, sorted_ref, delay_ref, wide_ref):
    band, observers, width = sorted_ref.shape
    size = weight_ref.shape[1]
    quants = width // size
    delay_ref[...] = jnp.full(delay_ref.shape, offset_ref[0, 0].astype(jnp.float32))
    wide_ref[...] = weight_ref[...].astype(jnp.float32)
    for k in range(band):
        for q in range(quants):
            lane = pl.ds(k * quants + q, observers, stride=band * quants)
            sorted_ref[k, :, q * size : (q + 1) * size] = wide_ref[lane, :].astype(jnp.bfloat16)


def band_sum(n_panel, quants, band, weight_ref, delay_ref, *refs):
    got_refs, (out_ref, lag_ref, shift_ref) = refs[:-3], refs[-3:]
    times, observers = out_ref.shape[1:]
    parts = n_panel
    size = got_refs[0].shape[2]
    span = parts * times
    held = [ref[...].astype(jnp.float32) for ref in got_refs]
    if held[0].shape[0] == parts:
        values = sum(held)
    else:
        n_obs = len(held)
        held = [jnp.sum(x.reshape(parts, n_obs, x.shape[1], size), axis=1) for x in held]
        me = lax.axis_index("obs")
        chunks = []
        for c in range(n_obs):
            chunk = held[0]
            for step in range(1, n_obs):
                chunk = jnp.where(lax.rem(me + (n_obs - step), n_obs) == c, held[step], chunk)
            chunks.append(chunk)
        values = jnp.concatenate(chunks, axis=1)
    flat = jnp.concatenate(
        [values[:, q * times : (q + 1) * times, :].reshape(span, size).astype(jnp.bfloat16) for q in range(quants)],
        axis=1,
    )
    total = None
    for k in range(band):
        one = lax.dot_general(flat, weight_ref[k], NT, preferred_element_type=jnp.float32)
        if k:
            lag_ref[k - 1, 0:8, :] = jnp.zeros((8, one.shape[1]), jnp.float32)
            lag_ref[k - 1, 8 : 8 + span, :] = one
            one = lag_ref[k - 1, 8 - k : 8 - k + span, :]
        total = one if total is None else total + one
    shift_ref[0:span, :] = jnp.zeros_like(total)
    shift_ref[span : 2 * span, :] = total
    moved = shift_ref[pl.ds(span - jnp.max(delay_ref[...]).astype(jnp.int32), span), :].reshape(parts, times, observers)
    slots = out_ref.shape[0] // parts
    if slots == 1:
        out_ref[...] = moved
    else:
        me = lax.axis_index("obs")
        for c in range(slots):
            mine = jnp.where(me == c, moved, 0.0).astype(out_ref.dtype)
            for p in range(parts):
                out_ref[p * slots + c] = mine[p]


def body(donor, donor_elem, local_coords, owner, weights, offsets):
    times, nodes, quants, elems = donor.shape
    points = local_coords.shape[1]
    every = owner.shape[0]
    n_panel = lax.axis_size("panel")
    n_obs = lax.axis_size("obs")
    size = every // n_panel
    observers, band = weights.shape[:2]
    rows = times * quants
    owner_row = owner.reshape(1, every)
    sources, pos = pl.pallas_call(
        functools.partial(interpolate, donor.shape, SHUFFLED, n_panel),
        out_shape=(pltpu.VMEM((rows, points), jnp.bfloat16), pltpu.VMEM((1, every), jnp.int32)),
        in_specs=[pl.BlockSpec(memory_space=pl.ANY)] * 4,
        out_specs=(VM, VM),
        scratch_shapes=[
            pltpu.VMEM((times * nodes * quants, elems), jnp.bfloat16),
            pltpu.VMEM((1, points), jnp.int32),
            pltpu.VMEM(local_coords.shape, jnp.float32),
            pltpu.VMEM((1, every), jnp.int32),
            pltpu.VMEM((times // 2, 8 * max(SHUFFLED, 1), elems), jnp.float32),
            pltpu.VMEM((2, 8 * ((nodes * quants + 7) // 8), 2 * LANES), jnp.float32),
            pltpu.VMEM((rows, points), jnp.float32),
            pltpu.SemaphoreType.DMA((5,)),
        ],
        name="interpolate",
    )(donor.reshape(times * nodes * quants, elems), donor_elem.reshape(1, points), local_coords, owner_row)
    outgoing = pl.pallas_call(
        functools.partial(place_own, n_panel),
        out_shape=pltpu.VMEM((n_panel, rows, size), jnp.bfloat16),
        in_specs=[VM, VM, VM],
        out_specs=VM,
        name="place_own",
    )(near(sources), near(owner_row), near(pos))
    if quants % n_obs == 0:
        outgoing = outgoing.reshape(n_panel * n_obs, rows // n_obs, size)
        got = lax.all_to_all(outgoing, ("panel", "obs"), split_axis=0, concat_axis=0, tiled=True)
    else:
        got = lax.all_to_all(outgoing, "panel", split_axis=0, concat_axis=0, tiled=True)
    others = [lax.ppermute(got, "obs", [(s, (s + step) % n_obs) for s in range(n_obs)]) for step in range(1, n_obs)]
    got, offsets = lax.optimization_barrier((got, offsets))
    weight_rows, delay = pl.pallas_call(
        sort_weights,
        out_shape=(
            pltpu.VMEM((band, observers, quants * size), jnp.bfloat16),
            pltpu.VMEM((1, LANES), jnp.float32),
        ),
        in_specs=[VM, VM, SM],
        out_specs=(VM, VM),
        scratch_shapes=[pltpu.VMEM((observers * band * quants, size), jnp.float32)],
        name="sort_weights",
    )(near(got), near(weights.reshape(observers * band * quants, size)), offsets)
    span = n_panel * times
    slots = n_obs if n_obs == 2 else 1
    partial = pl.pallas_call(
        functools.partial(band_sum, n_panel, quants, band),
        out_shape=pltpu.VMEM((n_panel * slots, times, observers), jnp.float32 if slots > 1 else jnp.float32),
        in_specs=[VM] * (2 + n_obs),
        out_specs=VM,
        scratch_shapes=[
            pltpu.VMEM((band - 1, 8 + span, observers), jnp.float32),
            pltpu.VMEM((2 * span, observers), jnp.float32),
        ],
        name="band_sum",
    )(near(weight_rows), near(delay), near(got), *[near(x) if n_obs == 2 else x for x in others])
    axes = ("panel", "obs") if slots > 1 else "panel"
    shares = lax.all_to_all(partial, axes, split_axis=0, concat_axis=0, tiled=True)
    return jnp.sum(shares.astype(jnp.float32), axis=0)


def solution(mesh):
    return jax.shard_map(
        body,
        mesh=mesh,
        in_specs=(
            P("panel", None, None, "obs"),
            P("obs"),
            P(None, "obs"),
            P(),
            P("obs", None, None, "panel"),
            P("obs", "panel"),
        ),
        out_specs=P("panel", "obs"),
        check_vma=False,
    )
```

```python
import functools

import jax
import jax.numpy as jnp
from jax import lax
from jax.experimental import pallas as pl
from jax.experimental.pallas import tpu as pltpu
from jax.sharding import PartitionSpec as P

LANES = 128
SHUFFLED = 36
NODE_SPOTS = (-1.0, -0.5, 0.0, 0.5, 1.0)
VM = pl.BlockSpec(memory_space=pltpu.VMEM)
SM = pl.BlockSpec(memory_space=pltpu.SMEM)
NT = (((1,), (1,)), ((), ()))


def near(x):
    return pltpu.with_memory_space_constraint(x, pltpu.VMEM)


def lagrange_rows(coords):
    rows = []
    for one in range(5):
        value = None
        scale = 1.0
        for two in range(5):
            if two != one:
                scale = scale * (NODE_SPOTS[one] - NODE_SPOTS[two])
                factor = coords - NODE_SPOTS[two]
                value = factor if value is None else value * factor
        rows.append(value * (1.0 / scale))
    return rows


def interpolate(shape, shuffled, n_panel, donor_src, elem_src, coords_src, owner_src, weight_src, out_ref, pos_ref, weight_ref, chunk_ref, elem_ref, coords_ref, owner_ref, wide_ref, table_ref, hold_ref, sems):
    times, nodes, quants, elems = shape
    points = coords_ref.shape[1]
    width = 2 * LANES
    rows = nodes * quants
    groups = (rows + 7) // 8
    pairs = times // 2
    half = pairs // 2 * 2 * rows
    copies = [
        pltpu.make_async_copy(donor_src.at[pl.ds(0, half), :], chunk_ref.at[pl.ds(0, half), :], sems.at[0]),
        pltpu.make_async_copy(
            donor_src.at[pl.ds(half, times * rows - half), :], chunk_ref.at[pl.ds(half, times * rows - half), :], sems.at[4]
        ),
    ]
    first = pltpu.make_async_copy(coords_src, coords_ref, sems.at[1])
    second = pltpu.make_async_copy(elem_src, elem_ref, sems.at[2])
    fourth = pltpu.make_async_copy(weight_src, weight_ref, sems.at[5])
    third = pltpu.make_async_copy(owner_src, owner_ref, sems.at[3])
    first.start()
    second.start()
    third.start()
    for copy in copies:
        copy.start()
    first.wait()
    second.wait()
    third.wait()
    rank_points(n_panel, owner_ref, pos_ref)
    base = lax.axis_index("obs") * elems
    upper = lax.broadcasted_iota(jnp.int32, (8, width), 0) >= quants
    tables = lagrange_rows(coords_ref[...])
    zero = jnp.zeros((8, width), jnp.float32)
    for tile in range(points // width):
        lanes = slice(tile * width, (tile + 1) * width)
        factors = [
            [jnp.broadcast_to(tables[a][d : d + 1, lanes], (8, width)) for a in range(5)] for d in range(3)
        ]
        ab = [factors[0][n // 5] * factors[1][n % 5] for n in range(25)]
        lasts = factors[2]
        mixed = {(c, (c + 1) % 5): jnp.where(upper, lasts[(c + 1) % 5], lasts[c]) for c in range(5)}
        for odd in range(2):
            for m in range(groups):
                low, high = 2 * m - odd, 2 * m - odd + 1
                if low < 0:
                    value = jnp.where(upper, ab[0] * lasts[0], zero)
                elif high >= nodes:
                    value = jnp.where(upper, zero, ab[-1] * lasts[-1])
                else:
                    front = ab[low // 5]
                    if high // 5 != low // 5:
                        front = jnp.where(upper, ab[high // 5], front)
                    value = front * mixed[(low % 5, high % 5)]
                table_ref[odd, m * 8 : m * 8 + 8, :] = value
        ids = elem_ref[0:1, lanes] - base
        wanted = jnp.broadcast_to(ids, (elems, width))
        pick = jnp.where(wanted == lax.broadcasted_iota(jnp.int32, (elems, width), 0), 1.0, 0.0).astype(jnp.bfloat16)
        for pair in range(pairs):
            if tile == 0 and pair == 0:
                for copy in copies:
                    copy.wait()
                fourth.start()
                if shuffled:
                    for p in range(pairs):
                        wide_ref[p] = chunk_ref[2 * rows * p : 2 * rows * p + 8 * shuffled, :].astype(jnp.float32)
            found = jnp.dot(
                chunk_ref[2 * rows * pair + 8 * shuffled : 2 * rows * (pair + 1), :], pick, preferred_element_type=jnp.float32)
            if shuffled:
                halves = [
                    jnp.take_along_axis(
                        wide_ref[pair],
                        jnp.broadcast_to(ids[:, h * LANES : (h + 1) * LANES], (8 * shuffled, LANES)),
                        axis=1,
                        mode="promise_in_bounds",
                    )
                    for h in range(2)
                ]
                found = jnp.concatenate([jnp.concatenate(halves, axis=1), found], axis=0)
            for odd in range(2):
                start = odd * (2 * rows - groups * 8)
                product = found[start : start + groups * 8, :] * table_ref[odd]
                total = jnp.sum(product.reshape(groups, 8, width), axis=0)
                total = total + pltpu.roll(total, 4, 0)
                for q in range(quants):
                    row = q * times + 2 * pair + odd
                    hold_ref[row : row + 1, lanes] = total[q : q + 1]
    out_ref[...] = hold_ref[...].astype(jnp.bfloat16)
    fourth.wait()


def place(owner_row, pos_row, src, n_panel, size):
    src = src.astype(jnp.float32)
    half = lax.shift_right_logical(owner_row, 1)
    picked = [jnp.where(half == p, src, 0.0).astype(jnp.bfloat16) for p in range(n_panel // 2)]
    spot = pos_row + (owner_row - 2 * half) * size
    hit = lax.broadcasted_iota(jnp.int32, (2 * size, spot.shape[1]), 0) == spot
    hot = jnp.where(hit, 1.0, 0.0).astype(jnp.bfloat16)
    return lax.dot_general(jnp.concatenate(picked, axis=0), hot, NT, preferred_element_type=jnp.float32)


def rank_points(n_panel, owner_ref, pos_ref):
    every = owner_ref.shape[1]
    tiles = every // LANES
    spans = (n_panel, LANES)
    rows_p = lax.broadcasted_iota(jnp.int32, spans, 0)
    hits = [
        jnp.where(rows_p == owner_ref[0:1, c * LANES : (c + 1) * LANES], 1.0, 0.0) for c in range(tiles)
    ]
    left = lax.broadcasted_iota(jnp.int32, (LANES, 2 * LANES), 0)
    right = lax.broadcasted_iota(jnp.int32, (LANES, 2 * LANES), 1)
    count = jnp.where((left < right), 1.0, 0.0).astype(jnp.bfloat16)
    sums = jnp.dot(
        jnp.concatenate(hits, axis=0).astype(jnp.bfloat16), count, preferred_element_type=jnp.float32
    )
    before = jnp.zeros(spans, jnp.float32)
    for c in range(tiles):
        part = sums[c * n_panel : (c + 1) * n_panel]
        rank = jnp.sum(hits[c] * (part[:, :LANES] + before), axis=0, keepdims=True)
        pos_ref[0:1, c * LANES : (c + 1) * LANES] = rank.astype(jnp.int32)
        before = before + part[:, LANES:]


def place_own(n_panel, src_ref, owner_ref, pos_ref, out_ref):
    rows, points = src_ref.shape
    size = owner_ref.shape[1] // n_panel
    at = pl.ds(pl.multiple_of(lax.axis_index("obs") * points, points), points)
    part = place(owner_ref[0:1, at], pos_ref[0:1, at], src_ref[...], n_panel, size).astype(jnp.bfloat16)
    for p in range(n_panel):
        out_ref[p] = part[p // 2 * rows : (p // 2 + 1) * rows, p % 2 * size : (p % 2 + 1) * size]


def sort_weights(got_ref, weight_ref, offset_ref, sorted_ref, delay_ref, wide_ref):
    band, observers, width = sorted_ref.shape
    size = weight_ref.shape[1]
    quants = width // size
    delay_ref[...] = jnp.full(delay_ref.shape, offset_ref[0, 0].astype(jnp.float32))
    wide_ref[...] = weight_ref[...].astype(jnp.float32)
    for k in range(band):
        for q in range(quants):
            lane = pl.ds(k * quants + q, observers, stride=band * quants)
            sorted_ref[k, :, q * size : (q + 1) * size] = wide_ref[lane, :].astype(jnp.bfloat16)


def band_sum(n_panel, quants, band, weight_ref, delay_ref, *refs):
    got_refs, (out_ref, lag_ref, shift_ref) = refs[:-3], refs[-3:]
    times, observers = out_ref.shape[1:]
    parts = n_panel
    size = got_refs[0].shape[2]
    span = parts * times
    held = [ref[...].astype(jnp.float32) for ref in got_refs]
    if held[0].shape[0] == parts:
        values = sum(held)
    else:
        n_obs = len(held)
        held = [jnp.sum(x.reshape(parts, n_obs, x.shape[1], size), axis=1) for x in held]
        me = lax.axis_index("obs")
        chunks = []
        for c in range(n_obs):
            chunk = held[0]
            for step in range(1, n_obs):
                chunk = jnp.where(lax.rem(me + (n_obs - step), n_obs) == c, held[step], chunk)
            chunks.append(chunk)
        values = jnp.concatenate(chunks, axis=1)
    flat = jnp.concatenate(
        [values[:, q * times : (q + 1) * times, :].reshape(span, size).astype(jnp.bfloat16) for q in range(quants)],
        axis=1,
    )
    total = None
    for k in range(band):
        one = lax.dot_general(flat, weight_ref[k], NT, preferred_element_type=jnp.float32)
        if k:
            lag_ref[k - 1, 0:8, :] = jnp.zeros((8, one.shape[1]), jnp.float32)
            lag_ref[k - 1, 8 : 8 + span, :] = one
            one = lag_ref[k - 1, 8 - k : 8 - k + span, :]
        total = one if total is None else total + one
    shift_ref[0:span, :] = jnp.zeros_like(total)
    shift_ref[span : 2 * span, :] = total
    moved = shift_ref[pl.ds(span - jnp.max(delay_ref[...]).astype(jnp.int32), span), :].reshape(parts, times, observers)
    slots = out_ref.shape[0] // parts
    if slots == 1:
        out_ref[...] = moved
    else:
        me = lax.axis_index("obs")
        for c in range(slots):
            mine = jnp.where(me == c, moved, 0.0).astype(out_ref.dtype)
            for p in range(parts):
                out_ref[p * slots + c] = mine[p]


def body(donor, donor_elem, local_coords, owner, weights, offsets):
    times, nodes, quants, elems = donor.shape
    points = local_coords.shape[1]
    every = owner.shape[0]
    n_panel = lax.axis_size("panel")
    n_obs = lax.axis_size("obs")
    size = every // n_panel
    observers, band = weights.shape[:2]
    rows = times * quants
    owner_row = owner.reshape(1, every)
    sources, pos, raw = pl.pallas_call(
        functools.partial(interpolate, donor.shape, SHUFFLED, n_panel),
        out_shape=(
            pltpu.VMEM((rows, points), jnp.bfloat16),
            pltpu.VMEM((1, every), jnp.int32),
            pltpu.VMEM((observers * band * quants, size), jnp.bfloat16),
        ),
        in_specs=[pl.BlockSpec(memory_space=pl.ANY)] * 5,
        out_specs=(VM, VM, VM),
        scratch_shapes=[
            pltpu.VMEM((times * nodes * quants, elems), jnp.bfloat16),
            pltpu.VMEM((1, points), jnp.int32),
            pltpu.VMEM(local_coords.shape, jnp.float32),
            pltpu.VMEM((1, every), jnp.int32),
            pltpu.VMEM((times // 2, 8 * max(SHUFFLED, 1), elems), jnp.float32),
            pltpu.VMEM((2, 8 * ((nodes * quants + 7) // 8), 2 * LANES), jnp.float32),
            pltpu.VMEM((rows, points), jnp.float32),
            pltpu.SemaphoreType.DMA((6,)),
        ],
        name="interpolate",
    )(donor.reshape(times * nodes * quants, elems), donor_elem.reshape(1, points), local_coords, owner_row, weights.reshape(observers * band * quants, size))
    outgoing = pl.pallas_call(
        functools.partial(place_own, n_panel),
        out_shape=pltpu.VMEM((n_panel, rows, size), jnp.bfloat16),
        in_specs=[VM, VM, VM],
        out_specs=VM,
        name="place_own",
    )(near(sources), near(owner_row), near(pos))
    if quants % n_obs == 0:
        outgoing = outgoing.reshape(n_panel * n_obs, rows // n_obs, size)
        got = lax.all_to_all(outgoing, ("panel", "obs"), split_axis=0, concat_axis=0, tiled=True)
    else:
        got = lax.all_to_all(outgoing, "panel", split_axis=0, concat_axis=0, tiled=True)
    others = [lax.ppermute(got, "obs", [(s, (s + step) % n_obs) for s in range(n_obs)]) for step in range(1, n_obs)]
    got, offsets = lax.optimization_barrier((got, offsets))
    weight_rows, delay = pl.pallas_call(
        sort_weights,
        out_shape=(
            pltpu.VMEM((band, observers, quants * size), jnp.bfloat16),
            pltpu.VMEM((1, LANES), jnp.float32),
        ),
        in_specs=[VM, VM, SM],
        out_specs=(VM, VM),
        scratch_shapes=[pltpu.VMEM((observers * band * quants, size), jnp.float32)],
        name="sort_weights",
    )(near(got), near(raw), offsets)
    span = n_panel * times
    slots = n_obs if n_obs == 2 else 1
    partial = pl.pallas_call(
        functools.partial(band_sum, n_panel, quants, band),
        out_shape=pltpu.VMEM((n_panel * slots, times, observers), jnp.float32 if slots > 1 else jnp.float32),
        in_specs=[VM] * (2 + n_obs),
        out_specs=VM,
        scratch_shapes=[
            pltpu.VMEM((band - 1, 8 + span, observers), jnp.float32),
            pltpu.VMEM((2 * span, observers), jnp.float32),
        ],
        name="band_sum",
    )(near(weight_rows), near(delay), near(got), *[near(x) if n_obs == 2 else x for x in others])
    axes = ("panel", "obs") if slots > 1 else "panel"
    shares = lax.all_to_all(partial, axes, split_axis=0, concat_axis=0, tiled=True)
    return jnp.sum(shares.astype(jnp.float32), axis=0)


def solution(mesh):
    return jax.shard_map(
        body,
        mesh=mesh,
        in_specs=(
            P("panel", None, None, "obs"),
            P("obs"),
            P(None, "obs"),
            P(),
            P("obs", None, None, "panel"),
            P("obs", "panel"),
        ),
        out_specs=P("panel", "obs"),
        check_vma=False,
    )
```
